32 devices in a mesh: ctx: 8 (over z, x), head: 4 (over y, core).
Axes of the slice: x: 2, y: 2, z: 4, core: 2. Of those that a mesh axis runs over, the one named last changes fastest.
Arguments:
- query: bfloat16 [16384, 8192], P(('ctx', 'head')), as said below
- key: bfloat16 [16384, 1024], P(('ctx', 'head')), as said below
- value: bfloat16 [16384, 1024], P(('ctx', 'head')), may hold values from -6 to 6
- doc_ids: int32 [128], replicated, may hold values from 0 to 20, never falling along the last dimension, each value on 1 to 8 neighbouring positions
- plan: int32 [128], replicated, may hold values from 0 to 127, as said below
Outputs:
- attended: bfloat16 [16384, 8192], P('ctx', 'head')
The draws below stay inside these ranges and needn't reach their ends.
Inputs may be any that keep to these rules, and one draw needn't show every extreme that they name: `doc_ids`: block ids never fall; each document holds 1 to 8 blocks, one exactly 8. `plan`: A permutation of the 128 blocks. Output positions k * 16 to (k + 1) * 16 - 1 belong to context shard k. Every shard receives 16 blocks; of the blocks j * 16 to (j + 1) * 16 - 1 at most 2 go to one shard, and exactly 2 to some shard. `query`: real values; no structure promised. `key`: real values; no structure promised.
All inputs are finite; a program needn't handle non-finite values.
Results may differ from the reference program's by a relative error of at most 0.0038.
Values may be sent and summed in bfloat16 or wider, within the bound.
A program may use at most 128 MiB of HBM per device.

```python
import math
import jax
import jax.numpy as jnp
import numpy as np
from jax import lax

HQ = 64
HK = 8
HD = 128
BLK = 128
BLK_DEV = 16
MAXDOC = 8
NBLK = 128
TOKENS = 16384
NDOC = 21


def key_field(key):
    base = jax.random.fold_in(key, 11)
    first = jax.random.fold_in(base, 0)
    field = jax.random.normal(first, (TOKENS, HK * HD), jnp.float32)
    marks = jnp.zeros((TOKENS,), bool)
    return (field, marks)


def draw_key(key, part):
    field, marks = key_field(key)
    return field.astype(jnp.bfloat16)


def draw_query(key, part):
    field, marks = key_field(key)
    noise_key = jax.random.fold_in(key, 12)
    noise = jax.random.normal(noise_key, (TOKENS, HQ * HD), jnp.float32)
    return jnp.where(marks[:, None], noise, noise).astype(jnp.bfloat16)


def draw_plan(key, part):
    base = jax.random.fold_in(key, 21)
    first, second, third, fourth = jax.random.split(base, 4)
    shards = NBLK // BLK_DEV
    ranks = jax.random.permutation(first, shards)
    offsets = ranks[jnp.arange(BLK_DEV) % shards]
    sigma = jax.random.permutation(second, shards)
    raw = jax.random.randint(third, (shards, BLK_DEV), 0, 1048576) * BLK_DEV + jnp.arange(BLK_DEV)[None, :]
    local_order = jnp.argsort(raw, axis=1, stable=True)
    sources = jnp.arange(shards)[:, None]
    target = sigma[(sources + offsets[local_order]) % shards]
    mixing = jax.random.permutation(fourth, NBLK)
    sort_key = target.reshape(NBLK) * NBLK + mixing
    return jnp.argsort(sort_key, stable=True).astype(jnp.int32)


def steps_of(stream_key, dims, cuts, low, high):
    def one(axis_at, blocks):
        draws = jax.random.uniform(jax.random.fold_in(jax.random.fold_in(stream_key, 6), axis_at), (blocks,), jnp.float32, low / len(cuts), high / len(cuts))
        return jnp.repeat(jnp.exp(draws), dims[axis_at] // blocks).reshape((-1,) + (1,) * (len(dims) - axis_at - 1))

    factor_of = one(*cuts[0])
    for cut in cuts[1:]:
        factor_of = factor_of * one(*cut)
    return factor_of


def length_profile(number_of, total, reach, lean):
    weights = [(1 << 20) // math.isqrt(rank ** lean) + 1 for rank in range(2, number_of + 1)]
    surplus, counts = total - reach - (number_of - 1), [1] * (number_of - 1)
    while surplus > 0:
        free = [i for i in range(number_of - 1) if counts[i] < reach]
        whole, budget = sum([weights[i] for i in free]), surplus
        for i in free:
            extra = min(reach - counts[i], max(1, budget * weights[i] // whole), surplus)
            counts[i] = counts[i] + extra
            surplus = surplus - extra
    return np.array([reach] + counts)


def uneven(rng, number_of, total, bound, lean):
    if number_of == 2:
        one = jax.random.randint(rng, (), max(1, total - bound), min(bound, total - 1) + 1)
        return jnp.stack([one, total - one])
    tallies = jnp.asarray(length_profile(number_of, total, bound, lean), jnp.int32)
    pairs = (number_of - 1) // 2
    giver, receiver = tallies[1:1 + 2 * pairs:2], tallies[2:2 + 2 * pairs:2]
    slack = jnp.minimum(giver - 1, bound - receiver)
    moved = jax.random.randint(jax.random.fold_in(rng, 1), (pairs,), 0, 1 << 20) % (slack + 1)
    tallies = tallies.at[1:1 + 2 * pairs:2].set(giver - moved).at[2:2 + 2 * pairs:2].set(receiver + moved)
    return tallies[jax.random.permutation(jax.random.fold_in(rng, 2), number_of)]


def bell_draw(key, extent, scale, most, cuts=(), held_as=jnp.bfloat16):
    drawn = jax.random.normal(key, extent, jnp.float32) * scale
    if len(cuts) > 0:
        drawn = steps_of(key, extent, cuts, -0.22, 0.18) * drawn
    return jnp.clip(drawn, min=-most, max=most).astype(held_as)


def setup_inputs(seed: int = 0) -> dict:
    streams_of = jax.random.split(jax.random.key(seed), 6)
    return {
        "query": draw_query(jax.random.fold_in(streams_of[5], 71), 0),
        "key": draw_key(jax.random.fold_in(streams_of[5], 71), 0),
        "value": bell_draw(streams_of[2], (TOKENS, HK * HD), 1.0, 6.0, ((0, 32),)),
        "doc_ids": jnp.searchsorted(jnp.cumsum(uneven(streams_of[3], NDOC, NBLK, MAXDOC, 2)), jnp.arange(NBLK), side="right").astype(jnp.int32),
        "plan": draw_plan(jax.random.fold_in(streams_of[5], 71), 0),
    }


def reference(query, key, value, doc_ids, plan):
    width = HQ * HD
    group = HQ // HK
    window = MAXDOC * BLK
    pad = (MAXDOC - 1) * BLK
    scale = 1.0 / math.sqrt(HD)
    key_pad = jnp.concatenate([jnp.zeros((pad, HK * HD), key.dtype), key], 0)
    value_pad = jnp.concatenate([jnp.zeros((pad, HK * HD), value.dtype), value], 0)
    row_docs = jnp.repeat(doc_ids, BLK)
    doc_pad = jnp.concatenate([jnp.full((pad,), -1, jnp.int32), row_docs.astype(jnp.int32)], 0)

    def one_block(block):
        start = (block * BLK).astype(jnp.int32)
        queries = lax.dynamic_slice_in_dim(query, start, BLK, 0).astype(jnp.float32).reshape(BLK, HK, group, HD)
        keys = lax.dynamic_slice_in_dim(key_pad, start, window, 0).astype(jnp.float32).reshape(window, HK, HD)
        values = lax.dynamic_slice_in_dim(value_pad, start, window, 0).astype(jnp.float32).reshape(window, HK, HD)
        docs = lax.dynamic_slice_in_dim(doc_pad, start, window, 0)
        scores = jnp.einsum('qkgd,skd->kgqs', queries, keys) * scale
        query_pos = start + jnp.arange(BLK, dtype=jnp.int32)
        key_pos = start - pad + jnp.arange(window, dtype=jnp.int32)
        allowed = (docs[None, :] == doc_ids[block]) & (key_pos[None, :] <= query_pos[:, None])
        scores = jnp.where(allowed, scores, -jnp.inf)
        top = lax.optimization_barrier(jnp.max(scores, axis=3, keepdims=True))
        expo = jnp.exp(scores - top)
        total = lax.optimization_barrier(jnp.sum(expo, axis=3))
        weights = lax.optimization_barrier(expo.astype(jnp.bfloat16)).astype(jnp.float32)
        summed = jnp.einsum('kgqs,skd->kgqd', weights, values)
        mixed = summed / total[..., None]
        return mixed.transpose(2, 0, 1, 3).reshape(BLK, width).astype(jnp.bfloat16)
    heads_out = lax.map(one_block, jnp.arange(NBLK, dtype=jnp.int32))
    return heads_out[plan].reshape(TOKENS, width)
```

```python
import functools
import math

import jax
import jax.numpy as jnp
from jax import lax
from jax.experimental import pallas as pl
from jax.experimental.pallas import tpu as pltpu
from jax.sharding import PartitionSpec as P

HD = 128
BLK = 128
MAXDOC = 8
CHUNKS = 4
ROW_HEADS = 2


def attend_kernel(heads, block_ref, count_ref, q_ref, k_ref, v_ref, o_ref):
    slot = pl.program_id(0)
    block = block_ref[slot]
    count = count_ref[slot]
    factor = math.log2(math.e) / math.sqrt(HD)
    rows = ROW_HEADS * BLK
    row_pos = lax.rem(lax.broadcasted_iota(jnp.int32, (rows, BLK), 0), BLK)
    causal = lax.broadcasted_iota(jnp.int32, (rows, BLK), 1) <= row_pos

    def body(pairs):
        width = 2 * pairs * BLK
        first = pl.multiple_of((block + MAXDOC - 2 * pairs) * BLK, BLK)
        keys = k_ref[pl.ds(first, width), :]
        values = v_ref[pl.ds(first, width), :]
        inside = jnp.full((rows, BLK), count - (2 * pairs - 1), jnp.int32) > 0
        for step in range(heads // ROW_HEADS):
            base = step * ROW_HEADS * HD
            queries = jnp.concatenate(
                [q_ref[:, base + i * HD : base + (i + 1) * HD] for i in range(ROW_HEADS)], axis=0
            )
            scores = lax.dot_general(
                queries, keys, (((1,), (1,)), ((), ())), preferred_element_type=jnp.float32
            )
            parts = [scores[:, i * BLK : (i + 1) * BLK] for i in range(2 * pairs)]
            parts[0] = jnp.where(inside, parts[0], -jnp.inf)
            parts[-1] = jnp.where(causal, parts[-1], -jnp.inf)
            top = functools.reduce(jnp.maximum, parts)
            top = jnp.max(top, axis=1, keepdims=True)
            parts = [jnp.exp2((part - top) * factor) for part in parts]
            total = jnp.sum(functools.reduce(jnp.add, parts), axis=1, keepdims=True)
            weights = jnp.concatenate([part.astype(jnp.bfloat16) for part in parts], axis=1)
            mixed = jnp.dot(weights, values, preferred_element_type=jnp.float32) / total
            mixed = mixed.astype(o_ref.dtype)
            for i in range(ROW_HEADS):
                o_ref[0, :, base + i * HD : base + (i + 1) * HD] = mixed[i * BLK : (i + 1) * BLK]

    for pairs in range(1, MAXDOC // 2 + 1):

        @pl.when((count + 1) // 2 == pairs)
        def _():
            body(pairs)


def attend(slot_block, slot_count, queries, keys, values, kv_head):
    slots = slot_block.shape[0]
    width = queries.shape[1]
    heads = width // HD
    window = keys.shape[0]
    flops = 4 * slots * heads * BLK * BLK * HD * 5
    return pl.pallas_call(
        functools.partial(attend_kernel, heads),
        out_shape=jax.ShapeDtypeStruct((slots, BLK, width), jnp.bfloat16),
        grid_spec=pltpu.PrefetchScalarGridSpec(
            num_scalar_prefetch=2,
            grid=(slots,),
            in_specs=[
                pl.BlockSpec((BLK, width), lambda s, b, n: (b[s], 0)),
                pl.BlockSpec((window, HD), lambda s, b, n: (0, kv_head)),
                pl.BlockSpec((window, HD), lambda s, b, n: (0, kv_head)),
            ],
            out_specs=pl.BlockSpec((1, BLK, width), lambda s, b, n: (s, 0, 0)),
        ),
        compiler_params=pltpu.CompilerParams(dimension_semantics=("arbitrary",)),
        cost_estimate=pl.CostEstimate(
            flops=flops, transcendentals=0, bytes_accessed=4 * queries.size + 4 * keys.size
        ),
        name="attend",
    )(slot_block, slot_count, queries, keys, values)


def place_kernel(slot_ref, x_ref, *rest):
    rest[-1][...] = x_ref[0]


def place(slot_of, received, so_far, chunk, chunks):
    blocks = slot_of.shape[0]
    width = received.shape[2]
    in_specs = [pl.BlockSpec((1, BLK, width), lambda i, s: (s[i], 0, 0))]
    operands = [slot_of, received]
    aliases = {}
    if so_far is not None:
        in_specs.append(pl.BlockSpec(memory_space=pl.ANY))
        operands.append(so_far)
        aliases = {2: 0}
    return pl.pallas_call(
        place_kernel,
        out_shape=jax.ShapeDtypeStruct((blocks * BLK, width * chunks), jnp.bfloat16),
        grid_spec=pltpu.PrefetchScalarGridSpec(
            num_scalar_prefetch=1,
            grid=(blocks,),
            in_specs=in_specs,
            out_specs=pl.BlockSpec((BLK, width), lambda i, s: (i, chunk)),
        ),
        compiler_params=pltpu.CompilerParams(dimension_semantics=("arbitrary",)),
        cost_estimate=pl.CostEstimate(
            flops=0, transcendentals=0, bytes_accessed=4 * blocks * BLK * width
        ),
        input_output_aliases=aliases,
        name="place",
    )(*operands)


def shifted(shard, axis, by):
    count = lax.axis_size(axis)
    pairs = [(i, i + by) for i in range(count) if 0 <= i + by < count]
    return lax.ppermute(shard, axis, pairs)


def shards(query, key, value, doc_ids, plan):
    head_count = lax.axis_size("head")
    shard_count = lax.axis_size("ctx")
    local_rows = query.shape[0]
    rows = head_count * local_rows
    blocks_here = rows // BLK
    q_width = query.shape[1] // head_count
    kv_width = key.shape[1] // head_count
    kv_heads = kv_width // HD
    width = q_width // CHUNKS
    per_kv = CHUNKS // kv_heads

    def exchange(parts):
        return lax.all_to_all(parts, "head", split_axis=0, concat_axis=0, tiled=True)

    kv = jnp.stack(
        [
            jnp.stack([x[:, h * kv_width : (h + 1) * kv_width] for x in (key, value)])
            for h in range(head_count)
        ]
    )
    kv = exchange(kv)
    kv = kv.transpose(1, 0, 2, 3).reshape(2, rows, kv_width)
    before = shifted(kv[:, rows - (MAXDOC - 1) * BLK :], "ctx", 1)

    shard = lax.axis_index("ctx")
    doc_start = jnp.sum((doc_ids[None, :] < doc_ids[:, None]).astype(jnp.int32), axis=1)
    counts = jnp.arange(doc_ids.shape[0], dtype=jnp.int32) - doc_start + 1
    own_counts = lax.dynamic_slice_in_dim(counts, shard * blocks_here, blocks_here)
    capacity = -(-blocks_here // shard_count)
    slots = shard_count * capacity
    grid = plan.reshape(shard_count, blocks_here)
    source = grid // blocks_here
    local = grid % blocks_here
    iota = jnp.arange(blocks_here, dtype=jnp.int32)
    lower = (iota[None, :] < iota[:, None])[None]
    rank = jnp.sum(
        ((source[:, :, None] == source[:, None, :]) & lower).astype(jnp.int32), axis=2
    )
    hit = (source == shard)[:, None, :] & (
        rank[:, None, :] == jnp.arange(capacity, dtype=jnp.int32)[None, :, None]
    )
    hit = hit.reshape(slots, blocks_here)
    local = jnp.broadcast_to(local[:, None, :], (shard_count, capacity, blocks_here))
    local = local.reshape(slots, blocks_here)
    slot_block = jnp.sum(jnp.where(hit, local, 0), axis=1)
    one_hot = hit[:, :, None] & (local[:, :, None] == iota[None, None, :])
    slot_count = jnp.sum(jnp.where(one_hot, own_counts[None, None, :], 0), axis=(1, 2))
    mine = lax.dynamic_index_in_dim(source * capacity + rank, shard, 0, False)

    window_k = jnp.concatenate([before[0], kv[0]], axis=0)
    window_v = jnp.concatenate([before[1], kv[1]], axis=0)

    result = None
    for chunk in range(CHUNKS):
        q = jnp.stack(
            [
                query[:, h * q_width + chunk * width : h * q_width + (chunk + 1) * width]
                for h in range(head_count)
            ]
        )
        q = exchange(q).reshape(rows, width)
        out = attend(slot_block, slot_count, q, window_k, window_v, chunk // per_kv)
        received = lax.all_to_all(out, "ctx", split_axis=0, concat_axis=0, tiled=True)
        result = place(mine, received, result, chunk, CHUNKS)
    return result


def solution(mesh):
    return jax.shard_map(
        shards,
        mesh=mesh,
        in_specs=(
            P(("ctx", "head"), None),
            P(("ctx", "head"), None),
            P(("ctx", "head"), None),
            P(),
            P(),
        ),
        out_specs=P("ctx", "head"),
        check_vma=False,
    )
```

```python
import functools
import math

import jax
import jax.numpy as jnp
from jax import lax
from jax.experimental import pallas as pl
from jax.experimental.pallas import tpu as pltpu
from jax.sharding import PartitionSpec as P

HD = 128
BLK = 128
MAXDOC = 8
ROW_HEADS = 2


def attend_kernel(heads, block_ref, count_ref, q_ref, k_ref, v_ref, o_ref):
    slot = pl.program_id(0)
    block = block_ref[slot]
    count = count_ref[slot]
    factor = math.log2(math.e) / math.sqrt(HD)
    rows = ROW_HEADS * BLK
    row_pos = lax.rem(lax.broadcasted_iota(jnp.int32, (rows, BLK), 0), BLK)
    causal = lax.broadcasted_iota(jnp.int32, (rows, BLK), 1) <= row_pos

    def body(pairs):
        width = 2 * pairs * BLK
        first = pl.multiple_of((block + MAXDOC - 2 * pairs) * BLK, BLK)
        keys = k_ref[pl.ds(first, width), :]
        values = v_ref[pl.ds(first, width), :]
        inside = jnp.full((rows, BLK), count - (2 * pairs - 1), jnp.int32) > 0
        for step in range(heads // ROW_HEADS):
            base = step * ROW_HEADS * HD
            queries = jnp.concatenate(
                [q_ref[:, base + i * HD : base + (i + 1) * HD] for i in range(ROW_HEADS)], axis=0
            )
            scores = lax.dot_general(
                queries, keys, (((1,), (1,)), ((), ())), preferred_element_type=jnp.float32
            )
            parts = [scores[:, i * BLK : (i + 1) * BLK] for i in range(2 * pairs)]
            parts[0] = jnp.where(inside, parts[0], -jnp.inf)
            parts[-1] = jnp.where(causal, parts[-1], -jnp.inf)
            top = functools.reduce(jnp.maximum, parts)
            top = jnp.max(top, axis=1, keepdims=True)
            parts = [jnp.exp2((part - top) * factor) for part in parts]
            total = jnp.sum(functools.reduce(jnp.add, parts), axis=1, keepdims=True)
            weights = jnp.concatenate([part.astype(jnp.bfloat16) for part in parts], axis=1)
            mixed = jnp.dot(weights, values, preferred_element_type=jnp.float32) / total
            mixed = mixed.astype(o_ref.dtype)
            for i in range(ROW_HEADS):
                o_ref[0, :, base + i * HD : base + (i + 1) * HD] = mixed[i * BLK : (i + 1) * BLK]

    for pairs in range(1, MAXDOC // 2 + 1):

        @pl.when((count + 1) // 2 == pairs)
        def _():
            body(pairs)


def attend(slot_block, slot_count, queries, window):
    slots = slot_block.shape[0]
    width = queries.shape[1]
    heads = width // HD
    span = window.shape[0]
    flops = 4 * slots * heads * BLK * BLK * HD * 5
    return pl.pallas_call(
        functools.partial(attend_kernel, heads),
        out_shape=jax.ShapeDtypeStruct((slots, BLK, width), jnp.bfloat16),
        grid_spec=pltpu.PrefetchScalarGridSpec(
            num_scalar_prefetch=2,
            grid=(slots,),
            in_specs=[
                pl.BlockSpec((BLK, width), lambda s, b, n: (b[s], 0)),
                pl.BlockSpec((span, HD), lambda s, b, n: (0, 0)),
                pl.BlockSpec((span, HD), lambda s, b, n: (0, 1)),
            ],
            out_specs=pl.BlockSpec((1, BLK, width), lambda s, b, n: (s, 0, 0)),
        ),
        compiler_params=pltpu.CompilerParams(dimension_semantics=("arbitrary",)),
        cost_estimate=pl.CostEstimate(
            flops=flops, transcendentals=0, bytes_accessed=4 * queries.size + 2 * window.size
        ),
        name="attend",
    )(slot_block, slot_count, queries, window, window)


def place_kernel(first, slot_ref, x_ref, *rest):
    o_ref, sems = rest[-2:]
    blocks = o_ref.shape[0] // BLK
    width = x_ref.shape[2]

    def copy(i):
        return pltpu.make_async_copy(
            x_ref.at[slot_ref[i]],
            o_ref.at[pl.ds(i * BLK, BLK), pl.ds(first, width)],
            sems.at[i],
        )

    for i in range(blocks):
        copy(i).start()
    for i in range(blocks):
        copy(i).wait()


def place(slot_of, received, so_far, first, full):
    blocks = slot_of.shape[0]
    width = received.shape[2]
    in_specs = [pl.BlockSpec(memory_space=pltpu.SMEM), pl.BlockSpec(memory_space=pltpu.VMEM)]
    operands = [slot_of, received]
    aliases = {}
    if so_far is not None:
        in_specs.append(pl.BlockSpec(memory_space=pl.ANY))
        operands.append(so_far)
        aliases = {2: 0}
    return pl.pallas_call(
        functools.partial(place_kernel, first),
        out_shape=jax.ShapeDtypeStruct((blocks * BLK, full), jnp.bfloat16),
        in_specs=in_specs,
        out_specs=pl.BlockSpec(memory_space=pl.ANY),
        scratch_shapes=[pltpu.SemaphoreType.DMA((blocks,))],
        cost_estimate=pl.CostEstimate(
            flops=0, transcendentals=0, bytes_accessed=4 * blocks * BLK * width
        ),
        input_output_aliases=aliases,
        name="place",
    )(*operands)


def shifted(shard, axis, by):
    count = lax.axis_size(axis)
    pairs = [(i, i + by) for i in range(count) if 0 <= i + by < count]
    return lax.ppermute(shard, axis, pairs)


def shards(query, key, value, doc_ids, plan):
    head_count = lax.axis_size("head")
    shard_count = lax.axis_size("ctx")
    local_rows = query.shape[0]
    rows = head_count * local_rows
    blocks_here = rows // BLK
    q_width = query.shape[1] // head_count
    kv_width = key.shape[1] // head_count
    kv_heads = kv_width // HD
    group = q_width // HD // kv_heads
    head = lax.axis_index("head")

    def pieces(kv_head, first, heads, with_kv, of_head):
        wanted = [(query, of_head * q_width + first * HD, heads * HD)]
        if with_kv:
            start = of_head * kv_width + kv_head * HD
            wanted += [(key, start, HD), (value, start, HD)]
        return wanted

    def all_pairs(wanted_of):
        parts = jnp.stack(
            [
                jnp.concatenate([x[:, s : s + w] for x, s, w in wanted_of(h)], axis=1)
                for h in range(head_count)
            ]
        )
        parts = lax.all_to_all(parts, "head", split_axis=0, concat_axis=0, tiled=True)
        return parts.reshape(rows, parts.shape[2])

    def by_permutes(wanted_of, after):
        xq, xk, xv, _ = lax.optimization_barrier((query, key, value, after))
        new = {id(query): xq, id(key): xk, id(value): xv}

        def part(of_head):
            return jnp.concatenate(
                [
                    lax.dynamic_slice(new[id(x)], (0, s), (local_rows, w))
                    for x, s, w in wanted_of(of_head)
                ],
                axis=1,
            )

        whole = None
        for step in range(head_count):
            other = jnp.bitwise_xor(head, step)
            piece = part(other)
            if step:
                piece = lax.ppermute(
                    piece, "head", [(h, h ^ step) for h in range(head_count)]
                )
            if whole is None:
                whole = jnp.zeros((rows, piece.shape[1]), piece.dtype)
            whole = lax.dynamic_update_slice(whole, piece, (other * local_rows, 0))
        return whole

    def windowed(kv):
        before = shifted(kv[rows - (MAXDOC - 1) * BLK :], "ctx", 1)
        return jnp.concatenate([before, kv], axis=0)

    shard = lax.axis_index("ctx")
    doc_start = jnp.sum((doc_ids[None, :] < doc_ids[:, None]).astype(jnp.int32), axis=1)
    counts = jnp.arange(doc_ids.shape[0], dtype=jnp.int32) - doc_start + 1
    own_counts = lax.dynamic_slice_in_dim(counts, shard * blocks_here, blocks_here)
    capacity = -(-blocks_here // shard_count)
    slots = shard_count * capacity
    grid = plan.reshape(shard_count, blocks_here)
    source = grid // blocks_here
    local = grid % blocks_here
    iota = jnp.arange(blocks_here, dtype=jnp.int32)
    lower = (iota[None, :] < iota[:, None])[None]
    rank = jnp.sum(
        ((source[:, :, None] == source[:, None, :]) & lower).astype(jnp.int32), axis=2
    )
    hit = (source == shard)[:, None, :] & (
        rank[:, None, :] == jnp.arange(capacity, dtype=jnp.int32)[None, :, None]
    )
    hit = hit.reshape(slots, blocks_here)
    local = jnp.broadcast_to(local[:, None, :], (shard_count, capacity, blocks_here))
    local = local.reshape(slots, blocks_here)
    slot_block = jnp.sum(jnp.where(hit, local, 0), axis=1)
    one_hot = hit[:, :, None] & (local[:, :, None] == iota[None, None, :])
    slot_count = jnp.sum(jnp.where(one_hot, own_counts[None, None, :], 0), axis=(1, 2))
    mine = lax.dynamic_index_in_dim(source * capacity + rank, shard, 0, False)

    chunks = []
    for kv_head in range(kv_heads):
        sizes = [group // 4, group // 4, group // 2] if kv_head == 0 else [group // 2] * 2
        start = kv_head * group
        for i, size in enumerate(sizes):
            chunks.append((kv_head, start, size, i == 0))
            start += size

    result = None
    window = None
    after = None
    arrived = []
    for at, (kv_head, first, heads, fresh) in enumerate(chunks):
        if at == 0:
            kv = all_pairs(
                lambda h: [(x, h * kv_width, HD) for x in (key, value)]
            )
            xq, kv = lax.optimization_barrier((query, kv))
            q = all_pairs(lambda h: [(xq, h * q_width, heads * HD)])
        else:
            both = by_permutes(
                functools.partial(pieces, kv_head, first, heads, fresh), after
            )
            q = both[:, : heads * HD]
            kv = both[:, heads * HD :]
        after = q[:8, :HD]
        arrived.append((kv_head, first, heads, q, windowed(kv) if fresh else None))
    for kv_head, first, heads, q, fresh_window in arrived:
        window = window if fresh_window is None else fresh_window
        out = attend(slot_block, slot_count, q, window)
        received = lax.all_to_all(out, "ctx", split_axis=0, concat_axis=0, tiled=True)
        result = place(mine, received, result, first * HD, q_width)
    return result


def solution(mesh):
    return jax.shard_map(
        shards,
        mesh=mesh,
        in_specs=(
            P(("ctx", "head"), None),
            P(("ctx", "head"), None),
            P(("ctx", "head"), None),
            P(),
            P(),
        ),
        out_specs=P("ctx", "head"),
        check_vma=False,
    )
```

```python
import functools
import math

import jax
import jax.numpy as jnp
from jax import lax
from jax.experimental import pallas as pl
from jax.experimental.pallas import tpu as pltpu
from jax.sharding import PartitionSpec as P


HD = 128
BLK = 128
MAXDOC = 8
ROW_HEADS = 2


def attend_kernel(heads, block_ref, count_ref, q_ref, kv_ref, o_ref):
    factor = math.log2(math.e) / math.sqrt(HD)
    rows = ROW_HEADS * BLK
    row_pos = lax.rem(lax.broadcasted_iota(jnp.int32, (rows, BLK), 0), BLK)
    causal = lax.broadcasted_iota(jnp.int32, (rows, BLK), 1) <= row_pos

    def body(pairs, slot, block, count):
        width = 2 * pairs * BLK
        first = pl.multiple_of((block + MAXDOC - 2 * pairs) * BLK, BLK)
        q_rows = pl.ds(pl.multiple_of(block * BLK, BLK), BLK)
        keys = kv_ref[pl.ds(first, width), :HD]
        values = kv_ref[pl.ds(first, width), HD:]
        inside = jnp.full((rows, BLK), count - (2 * pairs - 1), jnp.int32) > 0
        for step in range(heads // ROW_HEADS):
            base = step * ROW_HEADS * HD
            queries = jnp.concatenate(
                [q_ref[q_rows, base + i * HD : base + (i + 1) * HD] for i in range(ROW_HEADS)],
                axis=0,
            )
            scores = lax.dot_general(
                queries, keys, (((1,), (1,)), ((), ())), preferred_element_type=jnp.float32
            )
            parts = [scores[:, i * BLK : (i + 1) * BLK] for i in range(2 * pairs)]
            parts[0] = jnp.where(inside, parts[0], -jnp.inf)
            parts[-1] = jnp.where(causal, parts[-1], -jnp.inf)
            top = functools.reduce(jnp.maximum, parts)
            top = jnp.max(top, axis=1, keepdims=True)
            parts = [jnp.exp2((part - top) * factor) for part in parts]
            total = jnp.sum(functools.reduce(jnp.add, parts), axis=1, keepdims=True)
            weights = jnp.concatenate([part.astype(jnp.bfloat16) for part in parts], axis=1)
            mixed = jnp.dot(weights, values, preferred_element_type=jnp.float32) / total
            mixed = mixed.astype(o_ref.dtype)
            for i in range(ROW_HEADS):
                o_ref[slot, :, base + i * HD : base + (i + 1) * HD] = mixed[
                    i * BLK : (i + 1) * BLK
                ]

    def one(slot, carry):
        block = block_ref[slot]
        count = count_ref[slot]
        for pairs in range(1, MAXDOC // 2 + 1):

            @pl.when((count + 1) // 2 == pairs)
            def _():
                body(pairs, slot, block, count)

        return carry

    lax.fori_loop(0, o_ref.shape[0], one, 0)


def attend(slot_block, slot_count, queries, window):
    slots = slot_block.shape[0]
    width = queries.shape[1]
    heads = width // HD
    flops = 4 * slots * heads * BLK * BLK * HD * 5
    return pl.pallas_call(
        functools.partial(attend_kernel, heads),
        out_shape=jax.ShapeDtypeStruct((slots, BLK, width), jnp.bfloat16),
        in_specs=[pl.BlockSpec(memory_space=pltpu.SMEM)] * 2
        + [pl.BlockSpec(memory_space=pltpu.VMEM)] * 2,
        out_specs=pl.BlockSpec(memory_space=pltpu.VMEM),
        cost_estimate=pl.CostEstimate(
            flops=flops, transcendentals=0, bytes_accessed=4 * queries.size + 2 * window.size
        ),
        name="attend",
    )(slot_block, slot_count, queries, window)


def place_kernel(first, slot_ref, x_ref, *rest):
    o_ref, sems = rest[-2:]
    blocks = o_ref.shape[0] // BLK
    width = x_ref.shape[2]

    def copy(i):
        return pltpu.make_async_copy(
            x_ref.at[slot_ref[i]],
            o_ref.at[pl.ds(i * BLK, BLK), pl.ds(first, width)],
            sems.at[i],
        )

    for i in range(blocks):
        copy(i).start()
    for i in range(blocks):
        copy(i).wait()


def place(slot_of, received, so_far, first, full):
    blocks = slot_of.shape[0]
    width = received.shape[2]
    in_specs = [pl.BlockSpec(memory_space=pltpu.SMEM), pl.BlockSpec(memory_space=pltpu.VMEM)]
    operands = [slot_of, received]
    aliases = {}
    if so_far is not None:
        in_specs.append(pl.BlockSpec(memory_space=pl.ANY))
        operands.append(so_far)
        aliases = {2: 0}
    return pl.pallas_call(
        functools.partial(place_kernel, first),
        out_shape=jax.ShapeDtypeStruct((blocks * BLK, full), jnp.bfloat16),
        in_specs=in_specs,
        out_specs=pl.BlockSpec(memory_space=pl.ANY),
        scratch_shapes=[pltpu.SemaphoreType.DMA((blocks,))],
        cost_estimate=pl.CostEstimate(
            flops=0, transcendentals=0, bytes_accessed=4 * blocks * BLK * width
        ),
        input_output_aliases=aliases,
        name="place",
    )(*operands)


def shifted(shard, axis, by):
    count = lax.axis_size(axis)
    pairs = [(i, i + by) for i in range(count) if 0 <= i + by < count]
    return lax.ppermute(shard, axis, pairs)


def shards(query, key, value, doc_ids, plan):
    head_count = lax.axis_size("head")
    shard_count = lax.axis_size("ctx")
    local_rows = query.shape[0]
    rows = head_count * local_rows
    blocks_here = rows // BLK
    q_width = query.shape[1] // head_count
    kv_width = key.shape[1] // head_count
    kv_heads = kv_width // HD
    group = q_width // HD // kv_heads
    head = lax.axis_index("head")

    def pieces(kv_head, first, heads, with_kv, of_head):
        wanted = [(query, of_head * q_width + first * HD, heads * HD)]
        if with_kv:
            start = of_head * kv_width + kv_head * HD
            wanted += [(key, start, HD), (value, start, HD)]
        return wanted

    def all_pairs(wanted_of):
        parts = jnp.stack(
            [
                jnp.concatenate([x[:, s : s + w] for x, s, w in wanted_of(h)], axis=1)
                for h in range(head_count)
            ]
        )
        parts = lax.all_to_all(parts, "head", split_axis=0, concat_axis=0, tiled=True)
        return parts.reshape(rows, parts.shape[2])

    def by_permutes(wanted_of):
        def part(of_head):
            return jnp.concatenate(
                [
                    lax.dynamic_slice(x, (0, s), (local_rows, w))
                    for x, s, w in wanted_of(of_head)
                ],
                axis=1,
            )

        whole = None
        for step in range(head_count):
            other = jnp.bitwise_xor(head, step)
            piece = part(other)
            if step:
                piece = lax.ppermute(
                    piece, "head", [(h, h ^ step) for h in range(head_count)]
                )
            if whole is None:
                whole = jnp.zeros((rows, piece.shape[1]), piece.dtype)
            whole = lax.dynamic_update_slice(whole, piece, (other * local_rows, 0))
        return whole

    def windowed(kv):
        before = shifted(kv[rows - (MAXDOC - 1) * BLK :], "ctx", 1)
        return jnp.concatenate([before, kv], axis=0)

    shard = lax.axis_index("ctx")
    doc_start = jnp.sum((doc_ids[None, :] < doc_ids[:, None]).astype(jnp.int32), axis=1)
    counts = jnp.arange(doc_ids.shape[0], dtype=jnp.int32) - doc_start + 1
    own_counts = lax.dynamic_slice_in_dim(counts, shard * blocks_here, blocks_here)
    capacity = -(-blocks_here // shard_count)
    slots = shard_count * capacity
    grid = plan.reshape(shard_count, blocks_here)
    source = grid // blocks_here
    local = grid % blocks_here
    iota = jnp.arange(blocks_here, dtype=jnp.int32)
    lower = (iota[None, :] < iota[:, None])[None]
    rank = jnp.sum(
        ((source[:, :, None] == source[:, None, :]) & lower).astype(jnp.int32), axis=2
    )
    hit = (source == shard)[:, None, :] & (
        rank[:, None, :] == jnp.arange(capacity, dtype=jnp.int32)[None, :, None]
    )
    hit = hit.reshape(slots, blocks_here)
    local = jnp.broadcast_to(local[:, None, :], (shard_count, capacity, blocks_here))
    local = local.reshape(slots, blocks_here)
    slot_block = jnp.sum(jnp.where(hit, local, 0), axis=1)
    one_hot = hit[:, :, None] & (local[:, :, None] == iota[None, None, :])
    slot_count = jnp.sum(jnp.where(one_hot, own_counts[None, None, :], 0), axis=(1, 2))
    mine = lax.dynamic_index_in_dim(source * capacity + rank, shard, 0, False)

    chunks = []
    for kv_head in range(kv_heads):
        sizes = [group // 4, group // 4, group // 2] if kv_head == 0 else [group // 2] * 2
        start = kv_head * group
        for i, size in enumerate(sizes):
            chunks.append((kv_head, start, size, i == 0))
            start += size

    result = None
    window = None
    arrived = []
    for at, (kv_head, first, heads, fresh) in enumerate(chunks):
        if at == 0:
            kv = all_pairs(
                lambda h: [(x, h * kv_width, HD) for x in (key, value)]
            )
            q = all_pairs(lambda h: [(query, h * q_width, heads * HD)])
        else:
            both = by_permutes(functools.partial(pieces, kv_head, first, heads, fresh))
            q = both[:, : heads * HD]
            kv = both[:, heads * HD :]
        arrived.append((kv_head, first, heads, q, windowed(kv) if fresh else None))
    for kv_head, first, heads, q, fresh_window in arrived:
        window = window if fresh_window is None else fresh_window
        out = attend(slot_block, slot_count, q, window)
        received = lax.all_to_all(out, "ctx", split_axis=0, concat_axis=0, tiled=True)
        result = place(mine, received, result, first * HD, q_width)
    return result


def solution(mesh):
    return jax.shard_map(
        shards,
        mesh=mesh,
        in_specs=(
            P(("ctx", "head"), None),
            P(("ctx", "head"), None),
            P(("ctx", "head"), None),
            P(),
            P(),
        ),
        out_specs=P("ctx", "head"),
        check_vma=False,
    )
```

```python
import functools
import math

import jax
import jax.numpy as jnp
from jax import lax
from jax.experimental import pallas as pl
from jax.experimental.pallas import tpu as pltpu
from jax.sharding import PartitionSpec as P


HD = 128
BLK = 128
MAXDOC = 8
ROW_HEADS = 2


def attend_kernel(heads, block_ref, count_ref, q_ref, kv_ref, o_ref):
    factor = math.log2(math.e) / math.sqrt(HD)
    rows = ROW_HEADS * BLK
    row_pos = lax.rem(lax.broadcasted_iota(jnp.int32, (rows, BLK), 0), BLK)
    causal = lax.broadcasted_iota(jnp.int32, (rows, BLK), 1) <= row_pos

    def body(pairs, slot, block, count):
        width = 2 * pairs * BLK
        first = pl.multiple_of((block + MAXDOC - 2 * pairs) * BLK, BLK)
        q_rows = pl.ds(pl.multiple_of(block * BLK, BLK), BLK)
        keys = kv_ref[pl.ds(first, width), :HD]
        values = kv_ref[pl.ds(first, width), HD:]
        inside = jnp.full((rows, BLK), count - (2 * pairs - 1), jnp.int32) > 0
        all_scores = []
        for step in range(heads // ROW_HEADS):
            base = step * ROW_HEADS * HD
            queries = jnp.concatenate(
                [q_ref[q_rows, base + i * HD : base + (i + 1) * HD] for i in range(ROW_HEADS)],
                axis=0,
            )
            all_scores.append(
                lax.dot_general(
                    queries, keys, (((1,), (1,)), ((), ())), preferred_element_type=jnp.float32
                )
            )
        for step in range(heads // ROW_HEADS):
            base = step * ROW_HEADS * HD
            scores = all_scores[step]
            parts = [scores[:, i * BLK : (i + 1) * BLK] for i in range(2 * pairs)]
            parts[0] = jnp.where(inside, parts[0], -jnp.inf)
            parts[-1] = jnp.where(causal, parts[-1], -jnp.inf)
            top = functools.reduce(jnp.maximum, parts)
            top = jnp.max(top, axis=1, keepdims=True)
            parts = [jnp.exp2((part - top) * factor) for part in parts]
            total = jnp.sum(functools.reduce(jnp.add, parts), axis=1, keepdims=True)
            weights = jnp.concatenate([part.astype(jnp.bfloat16) for part in parts], axis=1)
            mixed = jnp.dot(weights, values, preferred_element_type=jnp.float32) / total
            mixed = mixed.astype(o_ref.dtype)
            for i in range(ROW_HEADS):
                o_ref[slot, :, base + i * HD : base + (i + 1) * HD] = mixed[
                    i * BLK : (i + 1) * BLK
                ]

    def one(slot, carry):
        block = block_ref[slot]
        count = count_ref[slot]
        for pairs in range(1, MAXDOC // 2 + 1):

            @pl.when((count + 1) // 2 == pairs)
            def _():
                body(pairs, slot, block, count)

        return carry

    lax.fori_loop(0, o_ref.shape[0], one, 0)


def attend(slot_block, slot_count, queries, window):
    slots = slot_block.shape[0]
    width = queries.shape[1]
    heads = width // HD
    flops = 4 * slots * heads * BLK * BLK * HD * 5
    return pl.pallas_call(
        functools.partial(attend_kernel, heads),
        out_shape=jax.ShapeDtypeStruct((slots, BLK, width), jnp.bfloat16),
        in_specs=[pl.BlockSpec(memory_space=pltpu.SMEM)] * 2
        + [pl.BlockSpec(memory_space=pltpu.VMEM)] * 2,
        out_specs=pl.BlockSpec(memory_space=pltpu.VMEM),
        cost_estimate=pl.CostEstimate(
            flops=flops, transcendentals=0, bytes_accessed=4 * queries.size + 2 * window.size
        ),
        name="attend",
    )(slot_block, slot_count, queries, window)


def place_kernel(first, slot_ref, x_ref, *rest):
    o_ref, sems = rest[-2:]
    blocks = o_ref.shape[0] // BLK
    width = x_ref.shape[2]

    def copy(i):
        return pltpu.make_async_copy(
            x_ref.at[slot_ref[i]],
            o_ref.at[pl.ds(i * BLK, BLK), pl.ds(first, width)],
            sems.at[i],
        )

    for i in range(blocks):
        copy(i).start()
    for i in range(blocks):
        copy(i).wait()


def place(slot_of, received, so_far, first, full):
    blocks = slot_of.shape[0]
    width = received.shape[2]
    in_specs = [pl.BlockSpec(memory_space=pltpu.SMEM), pl.BlockSpec(memory_space=pltpu.VMEM)]
    operands = [slot_of, received]
    aliases = {}
    if so_far is not None:
        in_specs.append(pl.BlockSpec(memory_space=pl.ANY))
        operands.append(so_far)
        aliases = {2: 0}
    return pl.pallas_call(
        functools.partial(place_kernel, first),
        out_shape=jax.ShapeDtypeStruct((blocks * BLK, full), jnp.bfloat16),
        in_specs=in_specs,
        out_specs=pl.BlockSpec(memory_space=pl.ANY),
        scratch_shapes=[pltpu.SemaphoreType.DMA((blocks,))],
        cost_estimate=pl.CostEstimate(
            flops=0, transcendentals=0, bytes_accessed=4 * blocks * BLK * width
        ),
        input_output_aliases=aliases,
        name="place",
    )(*operands)


def shifted(shard, axis, by):
    count = lax.axis_size(axis)
    pairs = [(i, i + by) for i in range(count) if 0 <= i + by < count]
    return lax.ppermute(shard, axis, pairs)


def shards(query, key, value, doc_ids, plan):
    head_count = lax.axis_size("head")
    shard_count = lax.axis_size("ctx")
    local_rows = query.shape[0]
    rows = head_count * local_rows
    blocks_here = rows // BLK
    q_width = query.shape[1] // head_count
    kv_width = key.shape[1] // head_count
    kv_heads = kv_width // HD
    group = q_width // HD // kv_heads
    head = lax.axis_index("head")

    def pieces(first, heads, fresh, of_head):
        wanted = [(query, of_head * q_width + first * HD, heads * HD)]
        if fresh is not None:
            start = of_head * kv_width + fresh * HD
            wanted += [(key, start, HD), (value, start, HD)]
        return wanted

    def all_pairs(wanted_of):
        parts = jnp.stack(
            [
                jnp.concatenate([x[:, s : s + w] for x, s, w in wanted_of(h)], axis=1)
                for h in range(head_count)
            ]
        )
        parts = lax.all_to_all(parts, "head", split_axis=0, concat_axis=0, tiled=True)
        return parts.reshape(rows, parts.shape[2])

    def by_permutes(wanted_of):
        def part(of_head):
            return jnp.concatenate(
                [
                    lax.dynamic_slice(x, (0, s), (local_rows, w))
                    for x, s, w in wanted_of(of_head)
                ],
                axis=1,
            )

        whole = None
        for step in range(head_count):
            other = jnp.bitwise_xor(head, step)
            piece = part(other)
            if step:
                piece = lax.ppermute(
                    piece, "head", [(h, h ^ step) for h in range(head_count)]
                )
            if whole is None:
                whole = jnp.zeros((rows, piece.shape[1]), piece.dtype)
            whole = lax.dynamic_update_slice(whole, piece, (other * local_rows, 0))
        return whole

    def windowed(kv):
        before = shifted(kv[rows - (MAXDOC - 1) * BLK :], "ctx", 1)
        return jnp.concatenate([before, kv], axis=0)

    shard = lax.axis_index("ctx")
    doc_start = jnp.sum((doc_ids[None, :] < doc_ids[:, None]).astype(jnp.int32), axis=1)
    counts = jnp.arange(doc_ids.shape[0], dtype=jnp.int32) - doc_start + 1
    own_counts = lax.dynamic_slice_in_dim(counts, shard * blocks_here, blocks_here)
    capacity = -(-blocks_here // shard_count)
    slots = shard_count * capacity
    grid = plan.reshape(shard_count, blocks_here)
    source = grid // blocks_here
    local = grid % blocks_here
    iota = jnp.arange(blocks_here, dtype=jnp.int32)
    lower = (iota[None, :] < iota[:, None])[None]
    rank = jnp.sum(
        ((source[:, :, None] == source[:, None, :]) & lower).astype(jnp.int32), axis=2
    )
    hit = (source == shard)[:, None, :] & (
        rank[:, None, :] == jnp.arange(capacity, dtype=jnp.int32)[None, :, None]
    )
    hit = hit.reshape(slots, blocks_here)
    local = jnp.broadcast_to(local[:, None, :], (shard_count, capacity, blocks_here))
    local = local.reshape(slots, blocks_here)
    slot_block = jnp.sum(jnp.where(hit, local, 0), axis=1)
    one_hot = hit[:, :, None] & (local[:, :, None] == iota[None, None, :])
    slot_count = jnp.sum(jnp.where(one_hot, own_counts[None, None, :], 0), axis=(1, 2))
    mine = lax.dynamic_index_in_dim(source * capacity + rank, shard, 0, False)

    chunks = []
    for kv_head in range(kv_heads):
        sizes = [group // 4, group // 4, group // 2] if kv_head == 0 else [group // 2] * 2
        start = kv_head * group
        for size in sizes:
            chunks.append((kv_head, start, size))
            start += size

    windows = {}
    arrived = []
    for at, (kv_head, first, heads) in enumerate(chunks):
        fresh = at if at < kv_heads else None
        if at == 0:
            kv = all_pairs(
                lambda h: [(x, h * kv_width, HD) for x in (key, value)]
            )
            q = all_pairs(lambda h: [(query, h * q_width, heads * HD)])
        else:
            both = by_permutes(functools.partial(pieces, first, heads, fresh))
            q = both[:, : heads * HD]
            kv = both[:, heads * HD :]
        if fresh is not None:
            windows[fresh] = windowed(kv)
        arrived.append(q)
    result = None
    for at, (kv_head, first, heads) in enumerate(chunks):
        out = attend(slot_block, slot_count, arrived[at], windows[kv_head])
        received = lax.all_to_all(out, "ctx", split_axis=0, concat_axis=0, tiled=True)
        result = place(mine, received, result, first * HD, q_width)
    return result


def solution(mesh):
    return jax.shard_map(
        shards,
        mesh=mesh,
        in_specs=(
            P(("ctx", "head"), None),
            P(("ctx", "head"), None),
            P(("ctx", "head"), None),
            P(),
            P(),
        ),
        out_specs=P("ctx", "head"),
        check_vma=False,
    )
```

```python
import functools
import math

import jax
import jax.numpy as jnp
from jax import lax
from jax.experimental import pallas as pl
from jax.experimental.pallas import tpu as pltpu
from jax.sharding import PartitionSpec as P


HD = 128
BLK = 128
MAXDOC = 8


def attend_kernel(heads, block_ref, count_ref, q_ref, kv_ref, o_ref):
    factor = math.log2(math.e) / math.sqrt(HD)
    row_heads = max(1, heads // 2)
    rows = row_heads * BLK
    row_pos = lax.rem(lax.broadcasted_iota(jnp.int32, (rows, BLK), 0), BLK)
    causal = lax.broadcasted_iota(jnp.int32, (rows, BLK), 1) <= row_pos

    def body(pairs, slot, block, count):
        width = 2 * pairs * BLK
        first = pl.multiple_of((block + MAXDOC - 2 * pairs) * BLK, BLK)
        q_rows = pl.ds(pl.multiple_of(block * BLK, BLK), BLK)
        keys = kv_ref[pl.ds(first, width), :HD]
        values = kv_ref[pl.ds(first, width), HD:]
        inside = jnp.full((rows, BLK), count - (2 * pairs - 1), jnp.int32) > 0
        all_scores = []
        for step in range(heads // row_heads):
            base = step * row_heads * HD
            queries = jnp.concatenate(
                [q_ref[q_rows, base + i * HD : base + (i + 1) * HD] for i in range(row_heads)],
                axis=0,
            )
            all_scores.append(
                lax.dot_general(
                    queries, keys, (((1,), (1,)), ((), ())), preferred_element_type=jnp.float32
                )
            )
        for step in range(heads // row_heads):
            base = step * row_heads * HD
            scores = all_scores[step]
            parts = [scores[:, i * BLK : (i + 1) * BLK] for i in range(2 * pairs)]
            parts[0] = jnp.where(inside, parts[0], -jnp.inf)
            parts[-1] = jnp.where(causal, parts[-1], -jnp.inf)
            top = functools.reduce(jnp.maximum, parts)
            top = jnp.max(top, axis=1, keepdims=True)
            parts = [jnp.exp2((part - top) * factor) for part in parts]
            total = jnp.sum(functools.reduce(jnp.add, parts), axis=1, keepdims=True)
            weights = jnp.concatenate([part.astype(jnp.bfloat16) for part in parts], axis=1)
            mixed = jnp.dot(weights, values, preferred_element_type=jnp.float32) / total
            mixed = mixed.astype(o_ref.dtype)
            for i in range(row_heads):
                o_ref[slot, :, base + i * HD : base + (i + 1) * HD] = mixed[
                    i * BLK : (i + 1) * BLK
                ]

    def one(slot, carry):
        block = block_ref[slot]
        count = count_ref[slot]
        for pairs in range(1, MAXDOC // 2 + 1):

            @pl.when((count + 1) // 2 == pairs)
            def _():
                body(pairs, slot, block, count)

        return carry

    lax.fori_loop(0, o_ref.shape[0], one, 0)


def attend(slot_block, slot_count, queries, window):
    slots = slot_block.shape[0]
    width = queries.shape[1]
    heads = width // HD
    flops = 4 * slots * heads * BLK * BLK * HD * 5
    return pl.pallas_call(
        functools.partial(attend_kernel, heads),
        out_shape=jax.ShapeDtypeStruct((slots, BLK, width), jnp.bfloat16),
        in_specs=[pl.BlockSpec(memory_space=pltpu.SMEM)] * 2
        + [pl.BlockSpec(memory_space=pltpu.VMEM)] * 2,
        out_specs=pl.BlockSpec(memory_space=pltpu.VMEM),
        cost_estimate=pl.CostEstimate(
            flops=flops, transcendentals=0, bytes_accessed=4 * queries.size + 2 * window.size
        ),
        name="attend",
    )(slot_block, slot_count, queries, window)


def place_kernel(first, slot_ref, x_ref, *rest):
    o_ref, sems = rest[-2:]
    blocks = o_ref.shape[0] // BLK
    width = x_ref.shape[2]

    def copy(i):
        return pltpu.make_async_copy(
            x_ref.at[slot_ref[i]],
            o_ref.at[pl.ds(i * BLK, BLK), pl.ds(first, width)],
            sems.at[i],
        )

    for i in range(blocks):
        copy(i).start()
    for i in range(blocks):
        copy(i).wait()


def place(slot_of, received, so_far, first, full):
    blocks = slot_of.shape[0]
    width = received.shape[2]
    in_specs = [pl.BlockSpec(memory_space=pltpu.SMEM), pl.BlockSpec(memory_space=pltpu.VMEM)]
    operands = [slot_of, received]
    aliases = {}
    if so_far is not None:
        in_specs.append(pl.BlockSpec(memory_space=pl.ANY))
        operands.append(so_far)
        aliases = {2: 0}
    return pl.pallas_call(
        functools.partial(place_kernel, first),
        out_shape=jax.ShapeDtypeStruct((blocks * BLK, full), jnp.bfloat16),
        in_specs=in_specs,
        out_specs=pl.BlockSpec(memory_space=pl.ANY),
        scratch_shapes=[pltpu.SemaphoreType.DMA((blocks,))],
        cost_estimate=pl.CostEstimate(
            flops=0, transcendentals=0, bytes_accessed=4 * blocks * BLK * width
        ),
        input_output_aliases=aliases,
        name="place",
    )(*operands)


def shifted(shard, axis, by):
    count = lax.axis_size(axis)
    pairs = [(i, i + by) for i in range(count) if 0 <= i + by < count]
    return lax.ppermute(shard, axis, pairs)


def shards(query, key, value, doc_ids, plan):
    head_count = lax.axis_size("head")
    shard_count = lax.axis_size("ctx")
    local_rows = query.shape[0]
    rows = head_count * local_rows
    blocks_here = rows // BLK
    q_width = query.shape[1] // head_count
    kv_width = key.shape[1] // head_count
    kv_heads = kv_width // HD
    group = q_width // HD // kv_heads
    head = lax.axis_index("head")

    def pieces(first, heads, fresh, of_head):
        wanted = [(query, of_head * q_width + first * HD, heads * HD)]
        if fresh is not None:
            start = of_head * kv_width + fresh * HD
            wanted += [(key, start, HD), (value, start, HD)]
        return wanted

    def all_pairs(wanted_of):
        parts = jnp.stack(
            [
                jnp.concatenate([x[:, s : s + w] for x, s, w in wanted_of(h)], axis=1)
                for h in range(head_count)
            ]
        )
        parts = lax.all_to_all(parts, "head", split_axis=0, concat_axis=0, tiled=True)
        return parts.reshape(rows, parts.shape[2])

    def by_permutes(wanted_of):
        def part(of_head):
            return jnp.concatenate(
                [
                    lax.dynamic_slice(x, (0, s), (local_rows, w))
                    for x, s, w in wanted_of(of_head)
                ],
                axis=1,
            )

        whole = None
        for step in range(head_count):
            other = jnp.bitwise_xor(head, step)
            piece = part(other)
            if step:
                piece = lax.ppermute(
                    piece, "head", [(h, h ^ step) for h in range(head_count)]
                )
            if whole is None:
                whole = jnp.zeros((rows, piece.shape[1]), piece.dtype)
            whole = lax.dynamic_update_slice(whole, piece, (other * local_rows, 0))
        return whole

    def windowed(kv):
        before = shifted(kv[rows - (MAXDOC - 1) * BLK :], "ctx", 1)
        return jnp.concatenate([before, kv], axis=0)

    shard = lax.axis_index("ctx")
    doc_start = jnp.sum((doc_ids[None, :] < doc_ids[:, None]).astype(jnp.int32), axis=1)
    counts = jnp.arange(doc_ids.shape[0], dtype=jnp.int32) - doc_start + 1
    own_counts = lax.dynamic_slice_in_dim(counts, shard * blocks_here, blocks_here)
    capacity = -(-blocks_here // shard_count)
    slots = shard_count * capacity
    grid = plan.reshape(shard_count, blocks_here)
    source = grid // blocks_here
    local = grid % blocks_here
    iota = jnp.arange(blocks_here, dtype=jnp.int32)
    lower = (iota[None, :] < iota[:, None])[None]
    rank = jnp.sum(
        ((source[:, :, None] == source[:, None, :]) & lower).astype(jnp.int32), axis=2
    )
    hit = (source == shard)[:, None, :] & (
        rank[:, None, :] == jnp.arange(capacity, dtype=jnp.int32)[None, :, None]
    )
    hit = hit.reshape(slots, blocks_here)
    local = jnp.broadcast_to(local[:, None, :], (shard_count, capacity, blocks_here))
    local = local.reshape(slots, blocks_here)
    slot_block = jnp.sum(jnp.where(hit, local, 0), axis=1)
    one_hot = hit[:, :, None] & (local[:, :, None] == iota[None, None, :])
    slot_count = jnp.sum(jnp.where(one_hot, own_counts[None, None, :], 0), axis=(1, 2))
    mine = lax.dynamic_index_in_dim(source * capacity + rank, shard, 0, False)

    chunks = []
    for kv_head in range(kv_heads):
        sizes = [group // 4, group // 4, group // 2] if kv_head == 0 else [group // 2] * 2
        start = kv_head * group
        for size in sizes:
            chunks.append((kv_head, start, size))
            start += size

    windows = {}
    arrived = []
    for at, (kv_head, first, heads) in enumerate(chunks):
        fresh = at if at < kv_heads else None
        if at == 0:
            kv = all_pairs(
                lambda h: [(x, h * kv_width, HD) for x in (key, value)]
            )
            q = all_pairs(lambda h: [(query, h * q_width, heads * HD)])
        else:
            both = by_permutes(functools.partial(pieces, first, heads, fresh))
            q = both[:, : heads * HD]
            kv = both[:, heads * HD :]
        if fresh is not None:
            windows[fresh] = windowed(kv)
        arrived.append(q)
    result = None
    for at, (kv_head, first, heads) in enumerate(chunks):
        out = attend(slot_block, slot_count, arrived[at], windows[kv_head])
        received = lax.all_to_all(out, "ctx", split_axis=0, concat_axis=0, tiled=True)
        result = place(mine, received, result, first * HD, q_width)
    return result


def solution(mesh):
    return jax.shard_map(
        shards,
        mesh=mesh,
        in_specs=(
            P(("ctx", "head"), None),
            P(("ctx", "head"), None),
            P(("ctx", "head"), None),
            P(),
            P(),
        ),
        out_specs=P("ctx", "head"),
        check_vma=False,
    )
```

```python
import functools
import math

import jax
import jax.numpy as jnp
from jax import lax
from jax.experimental import pallas as pl
from jax.experimental.pallas import tpu as pltpu
from jax.sharding import PartitionSpec as P


HD = 128
BLK = 128
MAXDOC = 8


def attend_kernel(heads, block_ref, count_ref, q_ref, kv_ref, o_ref, turned_ref):
    factor = math.log2(math.e) / math.sqrt(HD)
    row_heads = max(1, heads // 2)
    rows = row_heads * BLK
    row_pos = lax.rem(lax.broadcasted_iota(jnp.int32, (rows, BLK), 0), BLK)
    causal = lax.broadcasted_iota(jnp.int32, (rows, BLK), 1) <= row_pos

    def body(pairs, slot, block, count):
        width = 2 * pairs * BLK
        first = pl.multiple_of((block + MAXDOC - 2 * pairs) * BLK, BLK)
        q_rows = pl.ds(pl.multiple_of(block * BLK, BLK), BLK)
        keys = turned_ref[:, pl.ds(first, width)]
        values = kv_ref[pl.ds(first, width), HD:]
        inside = jnp.full((rows, BLK), count - (2 * pairs - 1), jnp.int32) > 0
        all_scores = []
        for step in range(heads // row_heads):
            base = step * row_heads * HD
            queries = jnp.concatenate(
                [q_ref[q_rows, base + i * HD : base + (i + 1) * HD] for i in range(row_heads)],
                axis=0,
            )
            all_scores.append(
                lax.dot_general(
                    queries, keys, (((1,), (0,)), ((), ())), preferred_element_type=jnp.float32
                )
            )
        for step in range(heads // row_heads):
            base = step * row_heads * HD
            scores = all_scores[step]
            parts = [scores[:, i * BLK : (i + 1) * BLK] for i in range(2 * pairs)]
            parts[0] = jnp.where(inside, parts[0], -jnp.inf)
            parts[-1] = jnp.where(causal, parts[-1], -jnp.inf)
            top = functools.reduce(jnp.maximum, parts)
            top = jnp.max(top, axis=1, keepdims=True)
            parts = [jnp.exp2((part - top) * factor) for part in parts]
            total = jnp.sum(functools.reduce(jnp.add, parts), axis=1, keepdims=True)
            weights = jnp.concatenate([part.astype(jnp.bfloat16) for part in parts], axis=1)
            mixed = jnp.dot(weights, values, preferred_element_type=jnp.float32) / total
            mixed = mixed.astype(o_ref.dtype)
            for i in range(row_heads):
                o_ref[slot, :, base + i * HD : base + (i + 1) * HD] = mixed[
                    i * BLK : (i + 1) * BLK
                ]

    def one(slot, carry):
        block = block_ref[slot]
        count = count_ref[slot]
        for pairs in range(1, MAXDOC // 2 + 1):

            @pl.when((count + 1) // 2 == pairs)
            def _():
                body(pairs, slot, block, count)

        return carry

    for i in range(kv_ref.shape[0] // BLK):
        turned_ref[:, i * BLK : (i + 1) * BLK] = kv_ref[i * BLK : (i + 1) * BLK, :HD].T
    lax.fori_loop(0, o_ref.shape[0], one, 0)


def attend(slot_block, slot_count, queries, window):
    slots = slot_block.shape[0]
    width = queries.shape[1]
    heads = width // HD
    flops = 4 * slots * heads * BLK * BLK * HD * 5
    return pl.pallas_call(
        functools.partial(attend_kernel, heads),
        out_shape=jax.ShapeDtypeStruct((slots, BLK, width), jnp.bfloat16),
        in_specs=[pl.BlockSpec(memory_space=pltpu.SMEM)] * 2
        + [pl.BlockSpec(memory_space=pltpu.VMEM)] * 2,
        out_specs=pl.BlockSpec(memory_space=pltpu.VMEM),
        scratch_shapes=[pltpu.VMEM((HD, window.shape[0]), jnp.bfloat16)],
        cost_estimate=pl.CostEstimate(
            flops=flops, transcendentals=0, bytes_accessed=4 * queries.size + 2 * window.size
        ),
        name="attend",
    )(slot_block, slot_count, queries, window)


def place_kernel(first, slot_ref, x_ref, *rest):
    o_ref, sems = rest[-2:]
    blocks = o_ref.shape[0] // BLK
    width = x_ref.shape[2]

    def copy(i):
        return pltpu.make_async_copy(
            x_ref.at[slot_ref[i]],
            o_ref.at[pl.ds(i * BLK, BLK), pl.ds(first, width)],
            sems.at[i],
        )

    for i in range(blocks):
        copy(i).start()
    for i in range(blocks):
        copy(i).wait()


def place(slot_of, received, so_far, first, full):
    blocks = slot_of.shape[0]
    width = received.shape[2]
    in_specs = [pl.BlockSpec(memory_space=pltpu.SMEM), pl.BlockSpec(memory_space=pltpu.VMEM)]
    operands = [slot_of, received]
    aliases = {}
    if so_far is not None:
        in_specs.append(pl.BlockSpec(memory_space=pl.ANY))
        operands.append(so_far)
        aliases = {2: 0}
    return pl.pallas_call(
        functools.partial(place_kernel, first),
        out_shape=jax.ShapeDtypeStruct((blocks * BLK, full), jnp.bfloat16),
        in_specs=in_specs,
        out_specs=pl.BlockSpec(memory_space=pl.ANY),
        scratch_shapes=[pltpu.SemaphoreType.DMA((blocks,))],
        cost_estimate=pl.CostEstimate(
            flops=0, transcendentals=0, bytes_accessed=4 * blocks * BLK * width
        ),
        input_output_aliases=aliases,
        name="place",
    )(*operands)


def shifted(shard, axis, by):
    count = lax.axis_size(axis)
    pairs = [(i, i + by) for i in range(count) if 0 <= i + by < count]
    return lax.ppermute(shard, axis, pairs)


def shards(query, key, value, doc_ids, plan):
    head_count = lax.axis_size("head")
    shard_count = lax.axis_size("ctx")
    local_rows = query.shape[0]
    rows = head_count * local_rows
    blocks_here = rows // BLK
    q_width = query.shape[1] // head_count
    kv_width = key.shape[1] // head_count
    kv_heads = kv_width // HD
    group = q_width // HD // kv_heads
    head = lax.axis_index("head")

    def pieces(first, heads, fresh, of_head):
        wanted = [(query, of_head * q_width + first * HD, heads * HD)]
        if fresh is not None:
            start = of_head * kv_width + fresh * HD
            wanted += [(key, start, HD), (value, start, HD)]
        return wanted

    def all_pairs(wanted_of):
        parts = jnp.stack(
            [
                jnp.concatenate([x[:, s : s + w] for x, s, w in wanted_of(h)], axis=1)
                for h in range(head_count)
            ]
        )
        parts = lax.all_to_all(parts, "head", split_axis=0, concat_axis=0, tiled=True)
        return parts.reshape(rows, parts.shape[2])

    def by_permutes(wanted_of):
        def part(of_head):
            return jnp.concatenate(
                [
                    lax.dynamic_slice(x, (0, s), (local_rows, w))
                    for x, s, w in wanted_of(of_head)
                ],
                axis=1,
            )

        whole = None
        for step in range(head_count):
            other = jnp.bitwise_xor(head, step)
            piece = part(other)
            if step:
                piece = lax.ppermute(
                    piece, "head", [(h, h ^ step) for h in range(head_count)]
                )
            if whole is None:
                whole = jnp.zeros((rows, piece.shape[1]), piece.dtype)
            whole = lax.dynamic_update_slice(whole, piece, (other * local_rows, 0))
        return whole

    def windowed(kv):
        before = shifted(kv[rows - (MAXDOC - 1) * BLK :], "ctx", 1)
        return jnp.concatenate([before, kv], axis=0)

    shard = lax.axis_index("ctx")
    doc_start = jnp.sum((doc_ids[None, :] < doc_ids[:, None]).astype(jnp.int32), axis=1)
    counts = jnp.arange(doc_ids.shape[0], dtype=jnp.int32) - doc_start + 1
    own_counts = lax.dynamic_slice_in_dim(counts, shard * blocks_here, blocks_here)
    capacity = -(-blocks_here // shard_count)
    slots = shard_count * capacity
    grid = plan.reshape(shard_count, blocks_here)
    source = grid // blocks_here
    local = grid % blocks_here
    iota = jnp.arange(blocks_here, dtype=jnp.int32)
    lower = (iota[None, :] < iota[:, None])[None]
    rank = jnp.sum(
        ((source[:, :, None] == source[:, None, :]) & lower).astype(jnp.int32), axis=2
    )
    hit = (source == shard)[:, None, :] & (
        rank[:, None, :] == jnp.arange(capacity, dtype=jnp.int32)[None, :, None]
    )
    hit = hit.reshape(slots, blocks_here)
    local = jnp.broadcast_to(local[:, None, :], (shard_count, capacity, blocks_here))
    local = local.reshape(slots, blocks_here)
    slot_block = jnp.sum(jnp.where(hit, local, 0), axis=1)
    one_hot = hit[:, :, None] & (local[:, :, None] == iota[None, None, :])
    slot_count = jnp.sum(jnp.where(one_hot, own_counts[None, None, :], 0), axis=(1, 2))
    mine = lax.dynamic_index_in_dim(source * capacity + rank, shard, 0, False)

    chunks = []
    for kv_head in range(kv_heads):
        sizes = [group // 4, group // 4, group // 2] if kv_head == 0 else [group // 2] * 2
        start = kv_head * group
        for size in sizes:
            chunks.append((kv_head, start, size))
            start += size

    windows = {}
    arrived = []
    for at, (kv_head, first, heads) in enumerate(chunks):
        fresh = at if at < kv_heads else None
        if at == 0:
            kv = all_pairs(
                lambda h: [(x, h * kv_width, HD) for x in (key, value)]
            )
            q = all_pairs(lambda h: [(query, h * q_width, heads * HD)])
        else:
            both = by_permutes(functools.partial(pieces, first, heads, fresh))
            q = both[:, : heads * HD]
            kv = both[:, heads * HD :]
        if fresh is not None:
            windows[fresh] = windowed(kv)
        arrived.append(q)
    result = None
    for at, (kv_head, first, heads) in enumerate(chunks):
        out = attend(slot_block, slot_count, arrived[at], windows[kv_head])
        received = lax.all_to_all(out, "ctx", split_axis=0, concat_axis=0, tiled=True)
        result = place(mine, received, result, first * HD, q_width)
    return result


def solution(mesh):
    return jax.shard_map(
        shards,
        mesh=mesh,
        in_specs=(
            P(("ctx", "head"), None),
            P(("ctx", "head"), None),
            P(("ctx", "head"), None),
            P(),
            P(),
        ),
        out_specs=P("ctx", "head"),
        check_vma=False,
    )
```
